32 devices in a mesh: dp: 8 (over y, x, core), seq: 4 (over z).
Axes of the slice: x: 2, y: 2, z: 4, core: 2. Of those that a mesh axis runs over, the one named last changes fastest.
Arguments:
- token_rows: bfloat16 [40960, 5120], P(('dp', 'seq')), may hold values from -6 to 6
- key_rows: bfloat16 [40960, 128], P(('dp', 'seq')), may hold values from -1.8 to 1.8
- query_rows: bfloat16 [40960, 128], P(('dp', 'seq')), may hold values from -0.1796875 to 0.1796875
- step_rows: bfloat16 [40960, 80], P(('dp', 'seq')), may hold values from -6 to 1000
- decay_log: float32 [80], replicated, may hold values from -9.3 to -1.8
- skip_gain: float32 [80], replicated, may hold values from 0.5 to 1.5
- source_rows: int32 [8, 5120], P('dp', 'seq'), may hold values from 0 to 40959, as said below
- document_starts: int32 [8, 6], P('dp'), may hold values from 0 to 5119, as said below
Outputs:
- layer_result_rows: bfloat16 [8, 5120, 5120], P('dp', 'seq')
The draws below stay inside these ranges and needn't reach their ends.
Inputs may be any that keep to these rules, and one draw needn't show every extreme that they name: `source_rows`: every loaded row is placed exactly once. The row at position p of a packed sequence is held by a device whose seq index is p // 1280. Positions come in aligned runs of 8 that hold consecutive rows of one device. A device takes at most 168 of its positions from any one device, and in every seq index some pair of devices reaches that number. `document_starts`: each row is strictly increasing and begins with 0.
All inputs are finite; a program needn't handle non-finite values.
Results may differ from the reference program's by a relative error of at most 0.0065.
Values may be sent and summed in bfloat16 or wider, within the bound.
A program may use at most 192 MiB of HBM per device.

```python
import math
import jax
import jax.numpy as jnp
from jax import lax

HEADS = 80
HEAD_DIM = 64
STATE = 128
SPAN = 256
SEG = 8
NDOC = 6
TOK_DEV = 1280
BINS = 8
LEN = 5120
ROWS = 40960
CAP = 168
WIDTH = 5120


def sudden_rows(key):
    hits = jax.random.randint(jax.random.fold_in(key, 11), (ROWS, 1), 0, max(LEN // 2, 2))
    return hits == 0


def draw_step_rows(key, part):
    offset_key = jax.random.fold_in(key, 21)
    rough_key = jax.random.fold_in(key, 22)
    start_offsets = jax.random.uniform(offset_key, (ROWS // TOK_DEV, 1), jnp.float32, -1.0, 1.0)
    start_offsets = jnp.repeat(start_offsets, TOK_DEV, axis=0)
    jitter_level = jnp.clip(jax.random.normal(rough_key, (ROWS, HEADS), jnp.float32), -4.0, 4.0)
    unscaled_steps = jnp.where(sudden_rows(key), 1000.0, -1.0 + start_offsets + jitter_level)
    return unscaled_steps.astype(jnp.bfloat16)


def draw_key_rows(key, part):
    base_key = jax.random.fold_in(key, 23)
    table_items = jnp.clip(0.3 * jax.random.normal(base_key, (ROWS, STATE), jnp.float32), -1.8, 1.8)
    table_items = jnp.where(sudden_rows(key), 0.002 * table_items, table_items)
    return table_items.astype(jnp.bfloat16)


def draw_decay_log(key, part):
    ranking = jax.random.permutation(jax.random.fold_in(key, 31), HEADS)
    slow_count = HEADS // 2
    slow_heads = ranking < slow_count
    spread = jax.random.uniform(jax.random.fold_in(key, 32), (HEADS,), jnp.float32, 0.0, 1.0)
    slow_log = math.log(0.0001) + spread * math.log(4.0)
    fast_log = math.log(0.05) + spread * math.log(3.0)
    return jnp.where(slow_heads, slow_log, fast_log).astype(jnp.float32)


def shuffle_segments(subkey):
    return jax.random.permutation(subkey, TOK_DEV // SEG)


def draw_source_rows(key, part):
    shard_number = LEN // TOK_DEV
    segment_count = TOK_DEV // SEG
    most_segments = CAP // SEG
    columns = []
    for column in range(shard_number):
        column_key = jax.random.fold_in(key, 100 + column)
        subkeys = jax.random.split(column_key, 6)
        heavy = jax.random.randint(subkeys[0], (), 0, BINS)
        offset_start = jax.random.randint(subkeys[1], (), 0, BINS - 1)
        others = (heavy + 1 + (offset_start + jnp.arange(segment_count - most_segments)) % (BINS - 1)) % BINS
        shifts = jnp.concatenate([jnp.full((most_segments,), heavy), others])
        first_perm = jax.random.permutation(subkeys[2], BINS)
        second_perm = jax.random.permutation(subkeys[3], BINS)
        sources = first_perm[(second_perm[:, None] + shifts[None, :]) % BINS]
        source_order = jax.vmap(shuffle_segments)(jax.random.split(subkeys[4], BINS))
        slot_order = jax.vmap(shuffle_segments)(jax.random.split(subkeys[5], BINS))
        source_at = jnp.take_along_axis(sources, slot_order, axis=1)
        segment_at = source_order[source_at, slot_order]
        inside = jnp.arange(SEG)
        row_start = (source_at * shard_number + column) * TOK_DEV + segment_at * SEG
        placed = row_start[:, :, None] + inside[None, None, :]
        columns.append(placed.reshape(BINS, TOK_DEV))
    return jnp.concatenate(columns, axis=1).astype(jnp.int32)


def pick_starts(subkey):
    chosen = jax.random.permutation(subkey, LEN - 1)[:NDOC - 1] + 1
    return jnp.sort(jnp.concatenate([jnp.zeros((1,), jnp.int32), chosen.astype(jnp.int32)]))


def draw_document_starts(key, part):
    return jax.vmap(pick_starts)(jax.random.split(jax.random.fold_in(key, 41), BINS))


def shard_levels(own_key, dims, cuts, least, high):
    level, own = 1.0, jax.random.fold_in(own_key, 6)
    for dim, shards_of in cuts:
        heights = jnp.exp(jax.random.uniform(jax.random.fold_in(own, dim), (shards_of,), jnp.float32, least / len(cuts), high / len(cuts)))
        level = level * jnp.repeat(heights, dims[dim] // shards_of).reshape([-1 if axis == dim else 1 for axis in range(len(dims))])
    return level


def scatter_about(own_key, extent, scale, reach, cuts=(), held_as=jnp.bfloat16):
    values = scale * jax.random.normal(own_key, extent, jnp.float32)
    if cuts:
        values = values * shard_levels(own_key, extent, cuts, -0.22, 0.18)
    return jnp.clip(values, -reach, reach).astype(held_as)


def setup_inputs(seed: int = 0) -> dict:
    splits = jax.random.split(jax.random.key(seed), 9)
    token_rows = scatter_about(splits[0], (ROWS, WIDTH), 1.0, 6.0, ((0, 32),))
    key_rows = draw_key_rows(jax.random.fold_in(splits[8], 71), 0)
    query_rows = scatter_about(splits[2], (ROWS, STATE), 0.03, 0.1796875, ((0, 32),))
    step_rows = draw_step_rows(jax.random.fold_in(splits[8], 71), 0)
    decay_log = draw_decay_log(jax.random.fold_in(splits[8], 71), 0)
    skip_gain = jnp.clip(jax.random.uniform(splits[5], (HEADS,), jnp.float32, 0.5, 1.5), 0.5, 1.5)
    source_rows = draw_source_rows(jax.random.fold_in(splits[8], 71), 0)
    document_starts = draw_document_starts(jax.random.fold_in(splits[8], 71), 0)
    return dict(token_rows=token_rows, key_rows=key_rows, query_rows=query_rows, step_rows=step_rows, decay_log=decay_log, skip_gain=skip_gain, source_rows=source_rows, document_starts=document_starts)


def span_pass(carried, pieces, decay_rate, skip_gain):
    values, keys_span, query_span, unscaled_steps, restart = pieces
    step_sizes = jax.nn.softplus(unscaled_steps.astype(jnp.float32))
    log_decay = -step_sizes * decay_rate[None, :]
    running_total = jnp.cumsum(log_decay, axis=0)
    document = jnp.cumsum(restart.astype(jnp.int32))
    position = jnp.arange(values.shape[0])
    linked = (document[:, None] == document[None, :]) & (position[None, :] <= position[:, None])
    scores = jnp.dot(query_span, keys_span.T, preferred_element_type=jnp.float32)
    decay_gap = running_total.T[:, :, None] - running_total.T[:, None, :]
    masked_gap = jnp.where(linked[None], decay_gap, -jnp.inf)
    weights = (scores[None] * jnp.exp(masked_gap) * step_sizes.T[:, None, :]).astype(jnp.bfloat16)
    within = jnp.einsum("hts,shp->thp", weights.astype(jnp.float32), values.astype(jnp.float32))
    entry_decay = jnp.where((document == 0)[:, None], jnp.exp(running_total), 0.0)
    from_state = jnp.einsum("tn,hnp->thp", query_span.astype(jnp.float32), carried,
                            precision=lax.Precision.HIGHEST) * entry_decay[:, :, None]
    to_end = running_total[-1][None, :] - running_total
    end_weight = jnp.where((document == document[-1])[:, None], jnp.exp(to_end), 0.0) * step_sizes
    scaled_values = (values.astype(jnp.float32) * end_weight[:, :, None]).astype(jnp.bfloat16)
    added_state = jnp.einsum("sn,shp->hnp", keys_span.astype(jnp.float32), scaled_values.astype(jnp.float32))
    retained = jnp.where(document[-1] == 0, jnp.exp(running_total[-1]), 0.0)
    carried = retained[:, None, None] * carried + added_state
    result = within + from_state + skip_gain[None, :, None] * values.astype(jnp.float32)
    return carried, result.astype(jnp.bfloat16)


def reference(token_rows, key_rows, query_rows, step_rows, decay_log, skip_gain, source_rows, document_starts):
    decay_rate = jnp.exp(decay_log)
    span_count = LEN // SPAN

    def advance(carried, pieces):
        return span_pass(carried, pieces, decay_rate, skip_gain)

    def one_sequence(inputs):
        wanted, starts = inputs
        values = jnp.take(token_rows, wanted, axis=0).reshape(span_count, SPAN, HEADS, HEAD_DIM)
        keys_packed = jnp.take(key_rows, wanted, axis=0).reshape(span_count, SPAN, STATE)
        query_packed = jnp.take(query_rows, wanted, axis=0).reshape(span_count, SPAN, STATE)
        steps_packed = jnp.take(step_rows, wanted, axis=0).reshape(span_count, SPAN, HEADS)
        position = jnp.arange(LEN)
        restart = jnp.any(position[:, None] == starts[None, :], axis=1).reshape(span_count, SPAN)
        zero_state = jnp.zeros((HEADS, STATE, HEAD_DIM), jnp.float32)
        final_state, results = lax.scan(advance, zero_state,
                                        (values, keys_packed, query_packed, steps_packed, restart))
        return results.reshape(LEN, HEADS * HEAD_DIM)

    return lax.map(one_sequence, (source_rows, document_starts))
```

```python
import functools

import jax
import jax.numpy as jnp
from jax import lax
from jax.experimental import pallas as pl
from jax.experimental.pallas import tpu as pltpu
from jax.sharding import PartitionSpec as P

SPAN = 256
SEG = 8
RUNS = SPAN // SEG
HALF = SPAN // 2
LANES = 128
CHUNK_HEADS = 16

f32, bf16 = jnp.float32, jnp.bfloat16
ANY = pl.BlockSpec(memory_space=pl.ANY)
VMEM_LIMIT = 60 * 1024 * 1024


def params(**more):
    return pltpu.CompilerParams(vmem_limit_bytes=VMEM_LIMIT, **more)


def whole(shape):
    return pl.BlockSpec(shape, lambda *_: (0,) * len(shape))


def spread(hilo, ones):
    return jnp.dot(hilo, ones, preferred_element_type=f32)


def split_float(value):
    high = value.astype(bf16)
    low = (value - high.astype(f32)).astype(bf16)
    return jnp.concatenate([high, low], axis=1)


def plan_kernel(groups, shards, runs, capacity, me_ref, wanted_ref, own_ref, send_ref, pick_ref):
    me = me_ref[0]
    earlier = lax.broadcasted_iota(jnp.int32, (runs, runs), 0) < lax.broadcasted_iota(
        jnp.int32, (runs, runs), 1
    )
    earlier = jnp.where(earlier, 1.0, 0.0).astype(bf16)

    def ranks(hit):
        ones = jnp.where(hit, 1.0, 0.0).astype(bf16)
        return jnp.dot(ones, earlier, preferred_element_type=f32).astype(jnp.int32)

    wanted = wanted_ref[...]
    mine = (wanted // runs) // shards == me
    local = wanted % runs
    rank = ranks(mine)
    lane = lax.broadcasted_iota(jnp.int32, (groups, LANES), 1)
    send = jnp.zeros((groups, LANES), jnp.int32)
    for slot in range(capacity):
        chosen = jnp.sum(jnp.where(mine & (rank == slot), local, 0), axis=1, keepdims=True)
        send = jnp.where(lane == slot, chosen, send)
    send_ref[...] = send
    source = (own_ref[...] // runs) // shards
    group = lax.broadcasted_iota(jnp.int32, (groups, runs), 0)
    hit = jnp.broadcast_to(source, (groups, runs)) == group
    pick_ref[...] = jnp.sum(
        jnp.where(hit, group * capacity + ranks(hit), 0), axis=0, keepdims=True
    )


def make_plan(groups, shards, runs, capacity, me, wanted, own):
    send, pick = pl.pallas_call(
        functools.partial(plan_kernel, groups, shards, runs, capacity),
        grid_spec=pltpu.PrefetchScalarGridSpec(
            num_scalar_prefetch=1,
            grid=(1,),
            in_specs=[whole((groups, runs)), whole((1, runs))],
            out_specs=[whole((groups, LANES)), whole((1, runs))],
        ),
        out_shape=[
            jax.ShapeDtypeStruct((groups, LANES), jnp.int32),
            jax.ShapeDtypeStruct((1, runs), jnp.int32),
        ],
        compiler_params=params(),
        name="plan",
    )(me, wanted, own)
    return send, pick[0]


def collect_kernel(groups, capacity, column, width, send_ref, rows_ref, token_ref, out_ref, held, gets, puts):
    def put(group):
        return pltpu.make_async_copy(held.at[group], out_ref.at[group], puts.at[group])

    for group in range(groups):

        @pl.loop(0, capacity)
        def _(slot):
            pltpu.make_async_copy(
                rows_ref.at[send_ref[group, slot], :, pl.ds(column, width)],
                held.at[group, slot],
                gets.at[group],
            ).start()

    for group in range(groups):
        pltpu.make_async_copy(held.at[group], held.at[group], gets.at[group]).wait()
        put(group).start()
    for group in range(groups):
        put(group).wait()


def collect(send, rows, token, groups, capacity, column, width):
    return pl.pallas_call(
        functools.partial(collect_kernel, groups, capacity, column, width),
        grid_spec=pltpu.PrefetchScalarGridSpec(
            num_scalar_prefetch=1,
            grid=(1,),
            in_specs=[ANY, ANY],
            out_specs=ANY,
            scratch_shapes=[
                pltpu.VMEM((groups, capacity, SEG, width), bf16),
                pltpu.SemaphoreType.DMA((groups,)),
                pltpu.SemaphoreType.DMA((groups,)),
            ],
        ),
        out_shape=jax.ShapeDtypeStruct((groups, capacity, SEG, width), bf16),
        compiler_params=params(),
        cost_estimate=pl.CostEstimate(
            flops=0, transcendentals=0, bytes_accessed=4 * groups * capacity * SEG * width
        ),
        name="collect",
    )(send, rows, token)


def fetch_spans(spans, pick_ref, source_ref, held, sems):
    @pl.when(pl.program_id(0) == 0)
    def _():
        @pl.loop(0, spans * RUNS)
        def _(run):
            pltpu.make_async_copy(
                source_ref.at[pick_ref[run]], held.at[run], sems.at[run // RUNS]
            ).start()


def fetched(held, sems, span):
    part = held.at[pl.ds(span * RUNS, RUNS)]
    pltpu.make_async_copy(part, part, sems.at[span]).wait()
    value = held[pl.ds(span * RUNS, RUNS)].astype(f32)
    return value.reshape(SPAN, value.shape[-1])


def prepare_kernel(
    spans, starts_count, pick_ref, starts_ref, small_ref, decay_ref,
    cum_ref, bias_ref, entry_ref, end_ref, device_ref, through_ref, keys_ref, query_ref, score_ref,
    held, sems, later,
):
    step = pl.program_id(0)
    span = spans - 1 - step

    @pl.when(step == 0)
    def _():
        @pl.loop(0, spans * RUNS)
        def _(run):
            pltpu.make_async_copy(
                small_ref.at[pick_ref[run]], held.at[run], sems.at[run // RUNS]
            ).start()

        later[...] = jnp.zeros_like(later)

    small = fetched(held, sems, span)
    keys = small[:, :LANES]
    query = small[:, LANES : 2 * LANES]
    raw = small[:, 2 * LANES :]
    steps = jnp.maximum(raw, 0.0) + jnp.log1p(jnp.exp(-jnp.abs(raw)))
    rate = jnp.exp(decay_ref[...])
    log_decay = -steps * rate
    row = lax.broadcasted_iota(jnp.int32, (SPAN, SPAN), 0)
    col = lax.broadcasted_iota(jnp.int32, (SPAN, SPAN), 1)
    lower = jnp.where(col <= row, 1.0, 0.0)
    cum = jnp.dot(lower, log_decay, precision=lax.Precision.HIGHEST, preferred_element_type=f32)
    low = span * SPAN
    doc_row = jnp.zeros((SPAN, SPAN), jnp.int32)
    doc_col = jnp.zeros((SPAN, SPAN), jnp.int32)
    doc = jnp.zeros((SPAN, LANES), jnp.int32)
    last = jnp.int32(0)
    after = jnp.int32(0)
    row_lanes = row[:, :LANES]
    for number in range(starts_count):
        start = starts_ref[number] - low
        inside = (start >= 0) & (start < SPAN)
        at = jnp.where(inside, start, jnp.int32(1 << 20))
        doc_row += (row >= at).astype(jnp.int32)
        doc_col += (col >= at).astype(jnp.int32)
        doc += (row_lanes >= at).astype(jnp.int32)
        last += inside.astype(jnp.int32)
        after += ((start >= SPAN) & (start < (spans - span) * SPAN)).astype(jnp.int32)
    linked = (doc_row == doc_col) & (col <= row)
    scores = lax.dot_general(
        query.astype(bf16), keys.astype(bf16), (((1,), (1,)), ((), ())), preferred_element_type=f32
    )
    score_ref[0] = jnp.where(linked, scores, 0.0)
    total = cum[SPAN - 1 :, :]
    to_end = total - cum
    entry_ref[...] = split_float(jnp.where(doc == 0, jnp.exp(cum), 0.0))
    at_end = doc == last
    end_ref[...] = split_float(jnp.where(at_end, jnp.exp(to_end), 0.0) * steps)
    reach = at_end & (after == 0)
    device_ref[...] = split_float(jnp.where(reach, jnp.exp(to_end + later[...]), 0.0) * steps)
    cum_ref[...] = cum
    bias_ref[...] = (jnp.log(steps) - cum).T
    keys_ref[...] = keys.T.astype(bf16)
    query_ref[...] = query.astype(bf16)
    later[...] = later[...] + total
    through_ref[...] = jnp.where(last + after == 0, jnp.exp(later[...]), 0.0)


def prepare(pick, starts, small, decay, tokens):
    spans = tokens // SPAN
    starts_count = starts.shape[0]

    def back(step, *_):
        return (spans - 1 - step, 0)

    def back_lanes(step, *_):
        return (0, spans - 1 - step)

    def rows(width):
        return pl.BlockSpec((SPAN, width), back)

    return pl.pallas_call(
        functools.partial(prepare_kernel, spans, starts_count),
        grid_spec=pltpu.PrefetchScalarGridSpec(
            num_scalar_prefetch=2,
            grid=(spans,),
            in_specs=[ANY, whole((1, LANES))],
            out_specs=[
                rows(LANES),
                pl.BlockSpec((LANES, SPAN), back_lanes),
                rows(2 * LANES),
                rows(2 * LANES),
                rows(2 * LANES),
                whole((1, LANES)),
                pl.BlockSpec((LANES, SPAN), back_lanes),
                rows(LANES),
                pl.BlockSpec((1, SPAN, SPAN), lambda step, *_: (spans - 1 - step, 0, 0)),
            ],
            scratch_shapes=[
                pltpu.VMEM((tokens // SEG, SEG, 3 * LANES), bf16),
                pltpu.SemaphoreType.DMA((spans,)),
                pltpu.VMEM((1, LANES), f32),
            ],
        ),
        out_shape=[
            jax.ShapeDtypeStruct((tokens, LANES), f32),
            jax.ShapeDtypeStruct((LANES, tokens), f32),
            jax.ShapeDtypeStruct((tokens, 2 * LANES), bf16),
            jax.ShapeDtypeStruct((tokens, 2 * LANES), bf16),
            jax.ShapeDtypeStruct((tokens, 2 * LANES), bf16),
            jax.ShapeDtypeStruct((1, LANES), f32),
            jax.ShapeDtypeStruct((LANES, tokens), bf16),
            jax.ShapeDtypeStruct((tokens, LANES), bf16),
            jax.ShapeDtypeStruct((spans, SPAN, SPAN), f32),
        ],
        compiler_params=params(),
        name="prepare",
    )(pick, starts, small, decay)


def state_kernel(spans, pick_ref, values_ref, keys_ref, device_ref, ones_ref, out_ref, held, sems):
    span = pl.program_id(0)
    fetch_spans(spans, pick_ref, values_ref, held, sems)

    @pl.when(span == 0)
    def _():
        out_ref[...] = jnp.zeros_like(out_ref)

    values = fetched(held, sems, span)
    scaled = (values * spread(device_ref[...], ones_ref[...])).astype(bf16)
    out_ref[...] += jnp.dot(keys_ref[...], scaled, preferred_element_type=f32)


def final_state(pick, values, keys, device, ones, tokens):
    spans = tokens // SPAN
    width = values.shape[-1]
    return pl.pallas_call(
        functools.partial(state_kernel, spans),
        grid_spec=pltpu.PrefetchScalarGridSpec(
            num_scalar_prefetch=1,
            grid=(spans,),
            in_specs=[
                ANY,
                pl.BlockSpec((LANES, SPAN), lambda s, *_: (0, s)),
                pl.BlockSpec((SPAN, 2 * LANES), lambda s, *_: (s, 0)),
                whole((2 * LANES, width)),
            ],
            out_specs=whole((LANES, width)),
            scratch_shapes=[
                pltpu.VMEM((tokens // SEG, SEG, width), bf16),
                pltpu.SemaphoreType.DMA((spans,)),
            ],
        ),
        out_shape=jax.ShapeDtypeStruct((LANES, width), f32),
        compiler_params=params(),
        cost_estimate=pl.CostEstimate(
            flops=6 * tokens * LANES * width, transcendentals=0, bytes_accessed=2 * tokens * width
        ),
        name="final_state",
    )(pick, values, keys, device, ones)


def layer_kernel(
    spans, first_head, heads, head_width, aliased, pick_ref, values_ref, cum_ref, bias_ref, entry_ref,
    end_ref, keys_ref, query_ref, score_ref, ones_ref, skip_ref, incoming_ref, *rest
):
    out_ref, held, sems, state, base = rest[1:] if aliased else rest
    span = pl.program_id(0)
    fetch_spans(spans, pick_ref, values_ref, held, sems)

    @pl.when(span == 0)
    def _():
        state[...] = incoming_ref[...]

    values = fetched(held, sems, span)
    ones = ones_ref[...]
    entry = spread(entry_ref[...], ones)
    from_state = jnp.dot(query_ref[...], state[...].astype(bf16), preferred_element_type=f32)
    base[...] = from_state * entry + skip_ref[...] * values
    scaled = (values * spread(end_ref[...], ones)).astype(bf16)
    added = jnp.dot(keys_ref[...], scaled, preferred_element_type=f32)
    state[...] = entry[SPAN - 1 :, :] * state[...] + added
    packed = values.astype(bf16)
    per_tile = LANES // head_width
    lane = lax.broadcasted_iota(jnp.int32, (HALF, LANES), 1) // head_width
    for tile in range(heads // per_tile):
        columns = slice(tile * LANES, (tile + 1) * LANES)
        for half in range(2):
            rows = slice(half * HALF, (half + 1) * HALF)
            depth = (half + 1) * HALF
            scores = score_ref[0, rows, :depth]
            total = None
            for inner in range(per_tile):
                head = first_head + tile * per_tile + inner
                gap = cum_ref[rows, head : head + 1] + bias_ref[head : head + 1, :depth]
                weights = (scores * jnp.exp(jnp.minimum(gap, 60.0))).astype(bf16)
                part = jnp.dot(weights, packed[:depth, columns], preferred_element_type=f32)
                total = part if total is None else jnp.where(lane == inner, part, total)
            out_ref[rows, columns] = (base[rows, columns] + total).astype(bf16)


def layer(result, pick, values, prepared, ones, skip, incoming, tokens, full, column, first_head, heads):
    cum, bias, entry, end, keys, query, scores = prepared
    spans = tokens // SPAN
    width = values.shape[-1]
    aliased = result is not None

    def rows(lanes):
        return pl.BlockSpec((SPAN, lanes), lambda s, *_: (s, 0))

    def lanes():
        return pl.BlockSpec((LANES, SPAN), lambda s, *_: (0, s))

    operands = [pick, values, cum, bias, entry, end, keys, query, scores, ones, skip, incoming]
    in_specs = [
        ANY, rows(LANES), lanes(), rows(2 * LANES), rows(2 * LANES), lanes(), rows(LANES),
        pl.BlockSpec((1, SPAN, SPAN), lambda s, *_: (s, 0, 0)),
        whole((2 * LANES, width)), whole((1, width)), whole((LANES, width)),
    ]
    if aliased:
        operands.append(result)
        in_specs.append(ANY)
    return pl.pallas_call(
        functools.partial(
            layer_kernel, spans, first_head, heads, width // heads, aliased
        ),
        grid_spec=pltpu.PrefetchScalarGridSpec(
            num_scalar_prefetch=1,
            grid=(spans,),
            in_specs=in_specs,
            out_specs=pl.BlockSpec((SPAN, width), lambda s, *_: (s, column // width)),
            scratch_shapes=[
                pltpu.VMEM((tokens // SEG, SEG, width), bf16),
                pltpu.SemaphoreType.DMA((spans,)),
                pltpu.VMEM((LANES, width), f32),
                pltpu.VMEM((SPAN, width), f32),
            ],
        ),
        out_shape=jax.ShapeDtypeStruct((tokens, full), bf16),
        input_output_aliases={len(operands) - 1: 0} if aliased else {},
        compiler_params=params(),
        cost_estimate=pl.CostEstimate(
            flops=8 * tokens * SPAN * width, transcendentals=tokens * SPAN * heads,
            bytes_accessed=4 * tokens * width,
        ),
        name="layer",
    )(*operands)


def shifted(block, axis, distance):
    devices = range(lax.axis_size(axis))
    route = [(i - distance, i) for i in devices if i - distance in devices]
    return lax.ppermute(block, axis, route)


def on_device(
    token_rows, key_rows, query_rows, step_rows, decay_log, skip_gain, source_rows, document_starts
):
    tokens, full = token_rows.shape
    groups = lax.axis_size("dp")
    shards = lax.axis_size("seq")
    heads = decay_log.shape[0]
    head_width = full // heads
    runs = tokens // SEG
    capacity = runs // groups + 1
    pad = LANES - heads

    own = source_rows[0].reshape(runs, SEG)[:, 0][None, :] // SEG
    wanted = lax.all_to_all(
        jnp.broadcast_to(own, (groups, runs)), "dp", split_axis=0, concat_axis=0, tiled=True
    )
    me = lax.axis_index("dp").astype(jnp.int32)[None]
    send, pick = make_plan(groups, shards, runs, capacity, me, wanted, own)

    small = jnp.concatenate([key_rows, query_rows, jnp.pad(step_rows, ((0, 0), (0, pad)))], axis=1)
    small = small.reshape(runs, SEG, 3 * LANES)
    values = token_rows.reshape(runs, SEG, full)

    def exchange(block):
        got = lax.all_to_all(block, "dp", split_axis=0, concat_axis=0, tiled=True)
        return got.reshape(groups * capacity, SEG, block.shape[-1])

    small_sent = collect(send, small, send, groups, capacity, 0, 3 * LANES)
    small_got = exchange(small_sent)

    chunk = CHUNK_HEADS
    count = heads // chunk
    width = chunk * head_width
    sent = []
    got = []
    for number in range(count):
        if number == 0:
            token = small_sent
        elif number == 1:
            token = sent[0]
        else:
            token = got[number - 2]
        block = collect(send, values, token, groups, capacity, number * width, width)
        sent.append(block)
        got.append(exchange(block))

    starts = document_starts[0] - lax.axis_index("seq").astype(jnp.int32) * tokens
    decay = jnp.pad(decay_log, (0, pad))[None, :]
    prepared = prepare(pick, starts, small_got, decay, tokens)
    cum, bias, entry, end, device, through, keys, query, scores = prepared
    lane_head = jnp.arange(full) // head_width
    ones = (jnp.arange(2 * LANES)[:, None] % LANES == lane_head[None, :]).astype(bf16)
    through = jnp.repeat(through[0, :heads], head_width)[None, :]
    skip = jnp.repeat(skip_gain, head_width)[None, :]

    incoming = []
    for number in range(count):
        part = slice(number * width, (number + 1) * width)
        final = final_state(pick, got[number], keys, device, ones[:, part], tokens)
        entering = jnp.zeros_like(final)
        for hop in range(shards - 1):
            outgoing = through[:, part] * entering + final
            entering = shifted(outgoing.astype(bf16), "seq", 1).astype(f32)
        incoming.append(entering)

    result = None
    for number in range(count):
        part = slice(number * width, (number + 1) * width)
        result = layer(
            result, pick, got[number], (cum, bias, entry, end, keys, query, scores),
            ones[:, part], skip[:, part], incoming[number], tokens, full, number * width,
            number * chunk, chunk,
        )
    return result[None]


def solution(mesh):
    in_specs = (
        P(("dp", "seq"), None),
        P(("dp", "seq"), None),
        P(("dp", "seq"), None),
        P(("dp", "seq"), None),
        P(),
        P(),
        P("dp", "seq"),
        P("dp", None),
    )
    out_specs = P("dp", "seq", None)
    return jax.shard_map(
        on_device, mesh=mesh, in_specs=in_specs, out_specs=out_specs, check_vma=False
    )
```

```python
import functools

import jax
import jax.numpy as jnp
from jax import lax
from jax.experimental import pallas as pl
from jax.experimental.pallas import tpu as pltpu
from jax.sharding import PartitionSpec as P

SPAN = 256
SEG = 8
RUNS = SPAN // SEG
HALF = SPAN // 2
LANES = 128

f32, bf16 = jnp.float32, jnp.bfloat16
ANY = pl.BlockSpec(memory_space=pl.ANY)
VMEM_LIMIT = 60 * 1024 * 1024


def params(**more):
    return pltpu.CompilerParams(vmem_limit_bytes=VMEM_LIMIT, **more)


def whole(shape):
    return pl.BlockSpec(shape, lambda *_: (0,) * len(shape))


def spread(hilo, ones):
    return jnp.dot(hilo, ones, preferred_element_type=f32)


def split_float(value):
    high = value.astype(bf16)
    low = (value - high.astype(f32)).astype(bf16)
    return jnp.concatenate([high, low], axis=1)


def plan_kernel(groups, shards, runs, capacity, me_ref, wanted_ref, own_ref, send_ref, pick_ref):
    me = me_ref[0]
    earlier = lax.broadcasted_iota(jnp.int32, (runs, runs), 0) < lax.broadcasted_iota(
        jnp.int32, (runs, runs), 1
    )
    earlier = jnp.where(earlier, 1.0, 0.0).astype(bf16)

    def ranks(hit):
        ones = jnp.where(hit, 1.0, 0.0).astype(bf16)
        return jnp.dot(ones, earlier, preferred_element_type=f32).astype(jnp.int32)

    wanted = wanted_ref[...]
    mine = (wanted // runs) // shards == me
    local = wanted % runs
    rank = ranks(mine)
    lane = lax.broadcasted_iota(jnp.int32, (groups, LANES), 1)
    send = jnp.zeros((groups, LANES), jnp.int32)
    for slot in range(capacity):
        chosen = jnp.sum(jnp.where(mine & (rank == slot), local, 0), axis=1, keepdims=True)
        send = jnp.where(lane == slot, chosen, send)
    send_ref[...] = send
    source = (own_ref[...] // runs) // shards
    group = lax.broadcasted_iota(jnp.int32, (groups, runs), 0)
    hit = jnp.broadcast_to(source, (groups, runs)) == group
    pick_ref[...] = jnp.sum(
        jnp.where(hit, group * capacity + ranks(hit), 0), axis=0, keepdims=True
    )


def make_plan(groups, shards, runs, capacity, me, wanted, own):
    send, pick = pl.pallas_call(
        functools.partial(plan_kernel, groups, shards, runs, capacity),
        grid_spec=pltpu.PrefetchScalarGridSpec(
            num_scalar_prefetch=1,
            grid=(1,),
            in_specs=[whole((groups, runs)), whole((1, runs))],
            out_specs=[whole((groups, LANES)), whole((1, runs))],
        ),
        out_shape=[
            jax.ShapeDtypeStruct((groups, LANES), jnp.int32),
            jax.ShapeDtypeStruct((1, runs), jnp.int32),
        ],
        compiler_params=params(),
        name="plan",
    )(me, wanted, own)
    return send, pick[0]


def collect_kernel(groups, capacity, parts, send_ref, token_ref, *rest):
    sources = rest[: len(parts)]
    out_ref, held, gets, puts = rest[len(parts) :]

    def put(group):
        return pltpu.make_async_copy(held.at[group], out_ref.at[group], puts.at[group])

    for group in range(groups):

        @pl.loop(0, capacity)
        def _(slot):
            place = 0
            for source, (column, width) in zip(sources, parts):
                pltpu.make_async_copy(
                    source.at[send_ref[group, slot], :, pl.ds(column, width)],
                    held.at[group, slot, :, pl.ds(place, width)],
                    gets.at[group],
                ).start()
                place += width

    for group in range(groups):
        pltpu.make_async_copy(held.at[group], held.at[group], gets.at[group]).wait()
        put(group).start()
    for group in range(groups):
        put(group).wait()


def collect(send, token, sources, parts, groups, capacity):
    width = sum(part[1] for part in parts)
    return pl.pallas_call(
        functools.partial(collect_kernel, groups, capacity, parts),
        grid_spec=pltpu.PrefetchScalarGridSpec(
            num_scalar_prefetch=1,
            grid=(1,),
            in_specs=[ANY] * (1 + len(sources)),
            out_specs=ANY,
            scratch_shapes=[
                pltpu.VMEM((groups, capacity, SEG, width), bf16),
                pltpu.SemaphoreType.DMA((groups,)),
                pltpu.SemaphoreType.DMA((groups,)),
            ],
        ),
        out_shape=jax.ShapeDtypeStruct((groups, capacity, SEG, width), bf16),
        compiler_params=params(),
        cost_estimate=pl.CostEstimate(
            flops=0, transcendentals=0, bytes_accessed=4 * groups * capacity * SEG * width
        ),
        name="collect",
    )(send, token, *sources)


def fetch_spans(spans, column, width, pick_ref, source_ref, held, sems):
    @pl.when(pl.program_id(0) == 0)
    def _():
        @pl.loop(0, spans * RUNS)
        def _(run):
            pltpu.make_async_copy(
                source_ref.at[pick_ref[run], :, pl.ds(column, width)],
                held.at[run],
                sems.at[run // RUNS],
            ).start()


def fetched(held, sems, span):
    part = held.at[pl.ds(span * RUNS, RUNS)]
    pltpu.make_async_copy(part, part, sems.at[span]).wait()
    value = held[pl.ds(span * RUNS, RUNS)].astype(f32)
    return value.reshape(SPAN, value.shape[-1])


def prepare_kernel(
    spans, starts_count, pick_ref, starts_ref, small_ref, decay_ref,
    cum_ref, bias_ref, entry_ref, end_ref, through_ref, keys_ref, query_ref, score_ref,
    held, sems, later,
):
    step = pl.program_id(0)
    span = spans - 1 - step

    fetch_spans(spans, 0, 3 * LANES, pick_ref, small_ref, held, sems)

    @pl.when(step == 0)
    def _():
        later[...] = jnp.zeros_like(later)

    small = fetched(held, sems, span)
    keys = small[:, :LANES]
    query = small[:, LANES : 2 * LANES]
    raw = small[:, 2 * LANES :]
    steps = jnp.maximum(raw, 0.0) + jnp.log1p(jnp.exp(-jnp.abs(raw)))
    rate = jnp.exp(decay_ref[...])
    log_decay = -steps * rate
    row = lax.broadcasted_iota(jnp.int32, (SPAN, SPAN), 0)
    col = lax.broadcasted_iota(jnp.int32, (SPAN, SPAN), 1)
    lower = jnp.where(col <= row, 1.0, 0.0)
    cum = jnp.dot(lower, log_decay, precision=lax.Precision.HIGHEST, preferred_element_type=f32)
    low = span * SPAN
    doc_row = jnp.zeros((SPAN, SPAN), jnp.int32)
    doc_col = jnp.zeros((SPAN, SPAN), jnp.int32)
    doc = jnp.zeros((SPAN, LANES), jnp.int32)
    last = jnp.int32(0)
    after = jnp.int32(0)
    row_lanes = row[:, :LANES]
    for number in range(starts_count):
        start = starts_ref[number] - low
        inside = (start >= 0) & (start < SPAN)
        at = jnp.where(inside, start, jnp.int32(1 << 20))
        doc_row += (row >= at).astype(jnp.int32)
        doc_col += (col >= at).astype(jnp.int32)
        doc += (row_lanes >= at).astype(jnp.int32)
        last += inside.astype(jnp.int32)
        after += ((start >= SPAN) & (start < (spans - span) * SPAN)).astype(jnp.int32)
    linked = (doc_row == doc_col) & (col <= row)
    scores = lax.dot_general(
        query.astype(bf16), keys.astype(bf16), (((1,), (1,)), ((), ())), preferred_element_type=f32
    )
    score_ref[0] = jnp.where(linked, scores, 0.0)
    total = cum[SPAN - 1 :, :]
    to_end = total - cum
    entry_ref[...] = split_float(jnp.where(doc == 0, jnp.exp(cum), 0.0))
    at_end = doc == last
    end_ref[...] = split_float(jnp.where(at_end, jnp.exp(to_end), 0.0) * steps)
    cum_ref[...] = cum
    bias_ref[...] = (jnp.log(steps) - cum).T
    keys_ref[...] = keys.T.astype(bf16)
    query_ref[...] = query.astype(bf16)
    later[...] = later[...] + total
    through_ref[...] = jnp.where(last + after == 0, jnp.exp(later[...]), 0.0)


def prepare(pick, starts, small, decay, tokens):
    spans = tokens // SPAN
    starts_count = starts.shape[0]

    def back(step, *_):
        return (spans - 1 - step, 0)

    def back_lanes(step, *_):
        return (0, spans - 1 - step)

    def rows(width):
        return pl.BlockSpec((SPAN, width), back)

    return pl.pallas_call(
        functools.partial(prepare_kernel, spans, starts_count),
        grid_spec=pltpu.PrefetchScalarGridSpec(
            num_scalar_prefetch=2,
            grid=(spans,),
            in_specs=[ANY, whole((1, LANES))],
            out_specs=[
                rows(LANES),
                pl.BlockSpec((LANES, SPAN), back_lanes),
                rows(2 * LANES),
                rows(2 * LANES),
                whole((1, LANES)),
                pl.BlockSpec((LANES, SPAN), back_lanes),
                rows(LANES),
                pl.BlockSpec((1, SPAN, SPAN), lambda step, *_: (spans - 1 - step, 0, 0)),
            ],
            scratch_shapes=[
                pltpu.VMEM((tokens // SEG, SEG, 3 * LANES), bf16),
                pltpu.SemaphoreType.DMA((spans,)),
                pltpu.VMEM((1, LANES), f32),
            ],
        ),
        out_shape=[
            jax.ShapeDtypeStruct((tokens, LANES), f32),
            jax.ShapeDtypeStruct((LANES, tokens), f32),
            jax.ShapeDtypeStruct((tokens, 2 * LANES), bf16),
            jax.ShapeDtypeStruct((tokens, 2 * LANES), bf16),
            jax.ShapeDtypeStruct((1, LANES), f32),
            jax.ShapeDtypeStruct((LANES, tokens), bf16),
            jax.ShapeDtypeStruct((tokens, LANES), bf16),
            jax.ShapeDtypeStruct((spans, SPAN, SPAN), f32),
        ],
        compiler_params=params(),
        name="prepare",
    )(pick, starts, small, decay)


def correct_kernel(
    result_ref, entry_ref, query_ref, ones_ref, incoming_ref, out_ref, reach
):
    @pl.when(pl.program_id(0) == 0)
    def _():
        reach[...] = jnp.ones_like(reach)

    entry = spread(entry_ref[...], ones_ref[...]) * reach[...]
    from_state = jnp.dot(query_ref[...], incoming_ref[...], preferred_element_type=f32)
    out_ref[...] = (result_ref[...].astype(f32) + from_state * entry).astype(bf16)
    reach[...] = entry[SPAN - 1 :, :]


def correct(result, entry, query, ones, incoming, column):
    tokens, full = result.shape
    width = incoming.shape[-1]

    def rows(lanes, block=0):
        return pl.BlockSpec((SPAN, lanes), lambda s: (s, block))

    return pl.pallas_call(
        correct_kernel,
        grid=(tokens // SPAN,),
        in_specs=[
            rows(width, column // width), rows(2 * LANES), rows(LANES),
            whole((2 * LANES, width)), whole((LANES, width)),
        ],
        out_specs=rows(width, column // width),
        scratch_shapes=[pltpu.VMEM((1, width), f32)],
        out_shape=jax.ShapeDtypeStruct((tokens, full), bf16),
        input_output_aliases={0: 0},
        compiler_params=params(),
        cost_estimate=pl.CostEstimate(
            flops=6 * tokens * LANES * width, transcendentals=0, bytes_accessed=4 * tokens * width
        ),
        name="correct",
    )(result, entry, query, ones, incoming)


def layer_kernel(
    spans, first_head, heads, head_width, lead, aliased, pick_ref, values_ref, cum_ref, bias_ref, entry_ref,
    end_ref, keys_ref, query_ref, score_ref, ones_ref, skip_ref, *rest
):
    out_ref, state, held, sems, base = rest[1:] if aliased else rest
    span = pl.program_id(0)
    fetch_spans(spans, lead, heads * head_width, pick_ref, values_ref, held, sems)

    @pl.when(span == 0)
    def _():
        state[...] = jnp.zeros_like(state)

    values = fetched(held, sems, span)
    ones = ones_ref[...]
    entry = spread(entry_ref[...], ones)
    from_state = jnp.dot(query_ref[...], state[...].astype(bf16), preferred_element_type=f32)
    base[...] = from_state * entry + skip_ref[...] * values
    scaled = (values * spread(end_ref[...], ones)).astype(bf16)
    added = jnp.dot(keys_ref[...], scaled, preferred_element_type=f32)
    state[...] = entry[SPAN - 1 :, :] * state[...] + added
    packed = values.astype(bf16)
    per_tile = LANES // head_width
    lane = lax.broadcasted_iota(jnp.int32, (HALF, LANES), 1) // head_width
    for tile in range(heads // per_tile):
        columns = slice(tile * LANES, (tile + 1) * LANES)
        for half in range(2):
            rows = slice(half * HALF, (half + 1) * HALF)
            depth = (half + 1) * HALF
            scores = score_ref[0, rows, :depth]
            total = None
            for inner in range(per_tile):
                head = first_head + tile * per_tile + inner
                gap = cum_ref[rows, head : head + 1] + bias_ref[head : head + 1, :depth]
                weights = (scores * jnp.exp(jnp.minimum(gap, 60.0))).astype(bf16)
                part = jnp.dot(weights, packed[:depth, columns], preferred_element_type=f32)
                total = part if total is None else jnp.where(lane == inner, part, total)
            out_ref[rows, columns] = (base[rows, columns] + total).astype(bf16)


def layer(result, pick, values, lead, prepared, ones, skip, tokens, full, column, first_head, heads):
    cum, bias, entry, end, keys, query, scores = prepared
    spans = tokens // SPAN
    width = ones.shape[-1]
    aliased = result is not None

    def rows(lanes):
        return pl.BlockSpec((SPAN, lanes), lambda s, *_: (s, 0))

    def lanes():
        return pl.BlockSpec((LANES, SPAN), lambda s, *_: (0, s))

    operands = [pick, values, cum, bias, entry, end, keys, query, scores, ones, skip]
    in_specs = [
        ANY, rows(LANES), lanes(), rows(2 * LANES), rows(2 * LANES), lanes(), rows(LANES),
        pl.BlockSpec((1, SPAN, SPAN), lambda s, *_: (s, 0, 0)),
        whole((2 * LANES, width)), whole((1, width)),
    ]
    if aliased:
        operands.append(result)
        in_specs.append(ANY)
    return pl.pallas_call(
        functools.partial(
            layer_kernel, spans, first_head, heads, width // heads, lead, aliased
        ),
        grid_spec=pltpu.PrefetchScalarGridSpec(
            num_scalar_prefetch=1,
            grid=(spans,),
            in_specs=in_specs,
            out_specs=[
                pl.BlockSpec((SPAN, width), lambda s, *_: (s, column // width)),
                whole((LANES, width)),
            ],
            scratch_shapes=[
                pltpu.VMEM((tokens // SEG, SEG, width), bf16),
                pltpu.SemaphoreType.DMA((spans,)),
                pltpu.VMEM((SPAN, width), f32),
            ],
        ),
        out_shape=[
            jax.ShapeDtypeStruct((tokens, full), bf16),
            jax.ShapeDtypeStruct((LANES, width), f32),
        ],
        input_output_aliases={len(operands) - 1: 0} if aliased else {},
        compiler_params=params(),
        cost_estimate=pl.CostEstimate(
            flops=8 * tokens * SPAN * width, transcendentals=tokens * SPAN * heads,
            bytes_accessed=4 * tokens * width,
        ),
        name="layer",
    )(*operands)


def chunk_plan(heads):
    unit = heads // 5
    return (2 * unit, 2 * unit, unit)


def shifted(block, axis, distance):
    devices = range(lax.axis_size(axis))
    route = [(i - distance, i) for i in devices if i - distance in devices]
    return lax.ppermute(block, axis, route)


def on_device(
    token_rows, key_rows, query_rows, step_rows, decay_log, skip_gain, source_rows, document_starts
):
    tokens, full = token_rows.shape
    groups = lax.axis_size("dp")
    shards = lax.axis_size("seq")
    heads = decay_log.shape[0]
    head_width = full // heads
    runs = tokens // SEG
    capacity = runs // groups + 1
    pad = LANES - heads

    own = source_rows[0].reshape(runs, SEG)[:, 0][None, :] // SEG
    wanted = lax.all_to_all(
        jnp.broadcast_to(own, (groups, runs)), "dp", split_axis=0, concat_axis=0, tiled=True
    )
    me = lax.axis_index("dp").astype(jnp.int32)[None]
    send, pick = make_plan(groups, shards, runs, capacity, me, wanted, own)

    small = jnp.concatenate([key_rows, query_rows, jnp.pad(step_rows, ((0, 0), (0, pad)))], axis=1)
    small = small.reshape(runs, SEG, 3 * LANES)
    values = token_rows.reshape(runs, SEG, full)

    def exchange(block):
        got = lax.all_to_all(block, "dp", split_axis=0, concat_axis=0, tiled=True)
        return got.reshape(groups * capacity, SEG, block.shape[-1])

    plan = chunk_plan(heads)
    blocks = []
    first = 0
    for count in plan:
        blocks.append((first, count, first * head_width, count * head_width))
        first += count
    lead = 3 * LANES

    def gathered(number, token):
        _, _, column, width = blocks[number]
        if number == 0:
            parts = ((0, lead), (column, width))
            return collect(send, token, (small, values), parts, groups, capacity)
        return collect(send, token, (values,), ((column, width),), groups, capacity)

    lane_head = jnp.arange(full) // head_width
    ones = (jnp.arange(2 * LANES)[:, None] % LANES == lane_head[None, :]).astype(bf16)
    skip = jnp.repeat(skip_gain, head_width)[None, :]
    starts = document_starts[0] - lax.axis_index("seq").astype(jnp.int32) * tokens
    decay = jnp.pad(decay_log, (0, pad))[None, :]

    sent = [gathered(0, send)]
    sent.append(gathered(1, sent[0]))
    result = None
    finals = []
    for number in range(len(blocks)):
        first_head, count, column, width = blocks[number]
        got = exchange(sent[number])
        if number == 0:
            prepared = prepare(pick, starts, got, decay, tokens)
            cum, bias, entry, end, through, keys, query, scores = prepared
            through = jnp.repeat(through[0, :heads], head_width)[None, :]
        part = slice(column, column + width)
        result, final = layer(
            result, pick, got, lead if number == 0 else 0,
            (cum, bias, entry, end, keys, query, scores),
            ones[:, part], skip[:, part], tokens, full, column, first_head, count,
        )
        finals.append(final)
        if number + 2 < len(blocks):
            sent.append(gathered(number + 2, final))

    for (first_head, count, column, width), final in zip(blocks, finals):
        part = slice(column, column + width)
        entering = shifted(final.astype(bf16), "seq", 1)
        for hop in range(shards - 2):
            outgoing = through[:, part] * entering.astype(f32) + final
            entering = shifted(outgoing.astype(bf16), "seq", 1)
        result = correct(result, entry, query, ones[:, part], entering, column)
    return result[None]


def solution(mesh):
    in_specs = (
        P(("dp", "seq"), None),
        P(("dp", "seq"), None),
        P(("dp", "seq"), None),
        P(("dp", "seq"), None),
        P(),
        P(),
        P("dp", "seq"),
        P("dp", None),
    )
    out_specs = P("dp", "seq", None)
    return jax.shard_map(
        on_device, mesh=mesh, in_specs=in_specs, out_specs=out_specs, check_vma=False
    )
```

```python
import functools

import jax
import jax.numpy as jnp
from jax import lax
from jax.experimental import pallas as pl
from jax.experimental.pallas import tpu as pltpu
from jax.sharding import PartitionSpec as P

SPAN = 256
SEG = 8
RUNS = SPAN // SEG
HALF = SPAN // 2
LANES = 128

f32, bf16 = jnp.float32, jnp.bfloat16
ANY = pl.BlockSpec(memory_space=pl.ANY)
VMEM_LIMIT = 60 * 1024 * 1024


def params(**more):
    return pltpu.CompilerParams(vmem_limit_bytes=VMEM_LIMIT, **more)


def whole(shape):
    return pl.BlockSpec(shape, lambda *_: (0,) * len(shape))


def spread(hilo, ones):
    return jnp.dot(hilo, ones, preferred_element_type=f32)


def split_float(value):
    high = value.astype(bf16)
    low = (value - high.astype(f32)).astype(bf16)
    return jnp.concatenate([high, low], axis=1)


def plan_kernel(groups, shards, runs, capacity, me_ref, wanted_ref, own_ref, send_ref, pick_ref):
    me = me_ref[0]
    earlier = lax.broadcasted_iota(jnp.int32, (runs, runs), 0) < lax.broadcasted_iota(
        jnp.int32, (runs, runs), 1
    )
    earlier = jnp.where(earlier, 1.0, 0.0).astype(bf16)

    def ranks(hit):
        ones = jnp.where(hit, 1.0, 0.0).astype(bf16)
        return jnp.dot(ones, earlier, preferred_element_type=f32).astype(jnp.int32)

    wanted = wanted_ref[...]
    mine = (wanted // runs) // shards == me
    local = wanted % runs
    rank = ranks(mine)
    lane = lax.broadcasted_iota(jnp.int32, (groups, LANES), 1)
    send = jnp.zeros((groups, LANES), jnp.int32)
    for slot in range(capacity):
        chosen = jnp.sum(jnp.where(mine & (rank == slot), local, 0), axis=1, keepdims=True)
        send = jnp.where(lane == slot, chosen, send)
    send_ref[...] = send
    source = (own_ref[...] // runs) // shards
    group = lax.broadcasted_iota(jnp.int32, (groups, runs), 0)
    hit = jnp.broadcast_to(source, (groups, runs)) == group
    pick_ref[...] = jnp.sum(
        jnp.where(hit, group * capacity + ranks(hit), 0), axis=0, keepdims=True
    )


def make_plan(groups, shards, runs, capacity, me, wanted, own):
    send, pick = pl.pallas_call(
        functools.partial(plan_kernel, groups, shards, runs, capacity),
        grid_spec=pltpu.PrefetchScalarGridSpec(
            num_scalar_prefetch=1,
            grid=(1,),
            in_specs=[whole((groups, runs)), whole((1, runs))],
            out_specs=[whole((groups, LANES)), whole((1, runs))],
        ),
        out_shape=[
            jax.ShapeDtypeStruct((groups, LANES), jnp.int32),
            jax.ShapeDtypeStruct((1, runs), jnp.int32),
        ],
        compiler_params=params(),
        name="plan",
    )(me, wanted, own)
    return send, pick[0]


def collect_kernel(groups, capacity, parts, send_ref, token_ref, *rest):
    sources = rest[: len(parts)]
    out_ref, held, gets, puts = rest[len(parts) :]

    def put(group):
        return pltpu.make_async_copy(held.at[group], out_ref.at[group], puts.at[group])

    for group in range(groups):

        @pl.loop(0, capacity)
        def _(slot):
            place = 0
            for source, (column, width) in zip(sources, parts):
                pltpu.make_async_copy(
                    source.at[send_ref[group, slot], :, pl.ds(column, width)],
                    held.at[group, slot, :, pl.ds(place, width)],
                    gets.at[group],
                ).start()
                place += width

    for group in range(groups):
        pltpu.make_async_copy(held.at[group], held.at[group], gets.at[group]).wait()
        put(group).start()
    for group in range(groups):
        put(group).wait()


def collect(send, token, sources, parts, groups, capacity):
    width = sum(part[1] for part in parts)
    return pl.pallas_call(
        functools.partial(collect_kernel, groups, capacity, parts),
        grid_spec=pltpu.PrefetchScalarGridSpec(
            num_scalar_prefetch=1,
            grid=(1,),
            in_specs=[ANY] * (1 + len(sources)),
            out_specs=ANY,
            scratch_shapes=[
                pltpu.VMEM((groups, capacity, SEG, width), bf16),
                pltpu.SemaphoreType.DMA((groups,)),
                pltpu.SemaphoreType.DMA((groups,)),
            ],
        ),
        out_shape=jax.ShapeDtypeStruct((groups, capacity, SEG, width), bf16),
        compiler_params=params(),
        cost_estimate=pl.CostEstimate(
            flops=0, transcendentals=0, bytes_accessed=4 * groups * capacity * SEG * width
        ),
        name="collect",
    )(send, token, *sources)


def fetch_spans(spans, column, width, pick_ref, source_ref, held, sems):
    @pl.when(pl.program_id(0) == 0)
    def _():
        @pl.loop(0, spans * RUNS)
        def _(run):
            pltpu.make_async_copy(
                source_ref.at[pick_ref[run], :, pl.ds(column, width)],
                held.at[run],
                sems.at[run // RUNS],
            ).start()


def fetched(held, sems, span):
    part = held.at[pl.ds(span * RUNS, RUNS)]
    pltpu.make_async_copy(part, part, sems.at[span]).wait()
    value = held[pl.ds(span * RUNS, RUNS)].astype(f32)
    return value.reshape(SPAN, value.shape[-1])


def prepare_kernel(
    spans, starts_count, pick_ref, starts_ref, small_ref, decay_ref,
    cum_ref, bias_ref, entry_ref, end_ref, through_ref, keys_ref, query_ref, score_ref,
    held, sems, later,
):
    step = pl.program_id(0)
    span = spans - 1 - step

    fetch_spans(spans, 0, 3 * LANES, pick_ref, small_ref, held, sems)

    @pl.when(step == 0)
    def _():
        later[...] = jnp.zeros_like(later)

    small = fetched(held, sems, span)
    keys = small[:, :LANES]
    query = small[:, LANES : 2 * LANES]
    raw = small[:, 2 * LANES :]
    steps = jnp.maximum(raw, 0.0) + jnp.log1p(jnp.exp(-jnp.abs(raw)))
    rate = jnp.exp(decay_ref[...])
    log_decay = -steps * rate
    row = lax.broadcasted_iota(jnp.int32, (SPAN, SPAN), 0)
    col = lax.broadcasted_iota(jnp.int32, (SPAN, SPAN), 1)
    lower = jnp.where(col <= row, 1.0, 0.0)
    cum = jnp.dot(lower, log_decay, precision=lax.Precision.HIGHEST, preferred_element_type=f32)
    low = span * SPAN
    doc_row = jnp.zeros((SPAN, SPAN), jnp.int32)
    doc_col = jnp.zeros((SPAN, SPAN), jnp.int32)
    doc = jnp.zeros((SPAN, LANES), jnp.int32)
    last = jnp.int32(0)
    after = jnp.int32(0)
    row_lanes = row[:, :LANES]
    for number in range(starts_count):
        start = starts_ref[number] - low
        inside = (start >= 0) & (start < SPAN)
        at = jnp.where(inside, start, jnp.int32(1 << 20))
        doc_row += (row >= at).astype(jnp.int32)
        doc_col += (col >= at).astype(jnp.int32)
        doc += (row_lanes >= at).astype(jnp.int32)
        last += inside.astype(jnp.int32)
        after += ((start >= SPAN) & (start < (spans - span) * SPAN)).astype(jnp.int32)
    linked = (doc_row == doc_col) & (col <= row)
    scores = lax.dot_general(
        query.astype(bf16), keys.astype(bf16), (((1,), (1,)), ((), ())), preferred_element_type=f32
    )
    score_ref[0] = jnp.where(linked, scores, 0.0)
    total = cum[SPAN - 1 :, :]
    to_end = total - cum
    entry_ref[...] = split_float(jnp.where(doc == 0, jnp.exp(cum), 0.0))
    at_end = doc == last
    end_ref[...] = split_float(jnp.where(at_end, jnp.exp(to_end), 0.0) * steps)
    cum_ref[...] = cum
    bias_ref[...] = (jnp.log(steps) - cum).T
    keys_ref[...] = keys.T.astype(bf16)
    query_ref[...] = query.astype(bf16)
    later[...] = later[...] + total
    through_ref[...] = jnp.where(last + after == 0, jnp.exp(later[...]), 0.0)


def prepare(pick, starts, small, decay, tokens):
    spans = tokens // SPAN
    starts_count = starts.shape[0]

    def back(step, *_):
        return (spans - 1 - step, 0)

    def back_lanes(step, *_):
        return (0, spans - 1 - step)

    def rows(width):
        return pl.BlockSpec((SPAN, width), back)

    return pl.pallas_call(
        functools.partial(prepare_kernel, spans, starts_count),
        grid_spec=pltpu.PrefetchScalarGridSpec(
            num_scalar_prefetch=2,
            grid=(spans,),
            in_specs=[ANY, whole((1, LANES))],
            out_specs=[
                rows(LANES),
                pl.BlockSpec((LANES, SPAN), back_lanes),
                rows(2 * LANES),
                rows(2 * LANES),
                whole((1, LANES)),
                pl.BlockSpec((LANES, SPAN), back_lanes),
                rows(LANES),
                pl.BlockSpec((1, SPAN, SPAN), lambda step, *_: (spans - 1 - step, 0, 0)),
            ],
            scratch_shapes=[
                pltpu.VMEM((tokens // SEG, SEG, 3 * LANES), bf16),
                pltpu.SemaphoreType.DMA((spans,)),
                pltpu.VMEM((1, LANES), f32),
            ],
        ),
        out_shape=[
            jax.ShapeDtypeStruct((tokens, LANES), f32),
            jax.ShapeDtypeStruct((LANES, tokens), f32),
            jax.ShapeDtypeStruct((tokens, 2 * LANES), bf16),
            jax.ShapeDtypeStruct((tokens, 2 * LANES), bf16),
            jax.ShapeDtypeStruct((1, LANES), f32),
            jax.ShapeDtypeStruct((LANES, tokens), bf16),
            jax.ShapeDtypeStruct((tokens, LANES), bf16),
            jax.ShapeDtypeStruct((spans, SPAN, SPAN), f32),
        ],
        compiler_params=params(),
        name="prepare",
    )(pick, starts, small, decay)


def correct_kernel(
    result_ref, entry_ref, query_ref, ones_ref, incoming_ref, out_ref, reach
):
    @pl.when(pl.program_id(0) == 0)
    def _():
        reach[...] = jnp.ones_like(reach)

    entry = spread(entry_ref[...], ones_ref[...]) * reach[...]
    from_state = jnp.dot(query_ref[...], incoming_ref[...], preferred_element_type=f32)
    out_ref[...] = (result_ref[...].astype(f32) + from_state * entry).astype(bf16)
    reach[...] = entry[SPAN - 1 :, :]


def correct(result, entry, query, ones, incoming, column):
    tokens, full = result.shape
    width = incoming.shape[-1]

    def rows(lanes, block=0):
        return pl.BlockSpec((SPAN, lanes), lambda s: (s, block))

    return pl.pallas_call(
        correct_kernel,
        grid=(tokens // SPAN,),
        in_specs=[
            rows(width, column // width), rows(2 * LANES), rows(LANES),
            whole((2 * LANES, width)), whole((LANES, width)),
        ],
        out_specs=rows(width, column // width),
        scratch_shapes=[pltpu.VMEM((1, width), f32)],
        out_shape=jax.ShapeDtypeStruct((tokens, full), bf16),
        input_output_aliases={0: 0},
        compiler_params=params(),
        cost_estimate=pl.CostEstimate(
            flops=6 * tokens * LANES * width, transcendentals=0, bytes_accessed=4 * tokens * width
        ),
        name="correct",
    )(result, entry, query, ones, incoming)


def layer_kernel(
    spans, first_head, heads, head_width, lead, aliased, pick_ref, values_ref, cum_ref, bias_ref, entry_ref,
    end_ref, keys_ref, query_ref, score_ref, ones_ref, skip_ref, *rest
):
    out_ref, state, held, sems, base = rest[1:] if aliased else rest
    span = pl.program_id(0)
    fetch_spans(spans, lead, heads * head_width, pick_ref, values_ref, held, sems)

    @pl.when(span == 0)
    def _():
        state[...] = jnp.zeros_like(state)

    values = fetched(held, sems, span)
    ones = ones_ref[...]
    entry = spread(entry_ref[...], ones)
    from_state = jnp.dot(query_ref[...], state[...].astype(bf16), preferred_element_type=f32)
    base[...] = from_state * entry + skip_ref[...] * values
    scaled = (values * spread(end_ref[...], ones)).astype(bf16)
    added = jnp.dot(keys_ref[...], scaled, preferred_element_type=f32)
    state[...] = entry[SPAN - 1 :, :] * state[...] + added
    packed = values.astype(bf16)
    per_tile = LANES // head_width
    lane = lax.broadcasted_iota(jnp.int32, (HALF, LANES), 1) // head_width
    for tile in range(heads // per_tile):
        columns = slice(tile * LANES, (tile + 1) * LANES)
        for half in range(2):
            rows = slice(half * HALF, (half + 1) * HALF)
            depth = (half + 1) * HALF
            scores = score_ref[0, rows, :depth]
            total = None
            for inner in range(per_tile):
                head = first_head + tile * per_tile + inner
                gap = cum_ref[rows, head : head + 1] + bias_ref[head : head + 1, :depth]
                weights = (scores * jnp.exp(jnp.minimum(gap, 60.0))).astype(bf16)
                part = jnp.dot(weights, packed[:depth, columns], preferred_element_type=f32)
                total = part if total is None else jnp.where(lane == inner, part, total)
            out_ref[rows, columns] = (base[rows, columns] + total).astype(bf16)


def layer(result, pick, values, lead, prepared, ones, skip, tokens, full, column, first_head, heads):
    cum, bias, entry, end, keys, query, scores = prepared
    spans = tokens // SPAN
    width = ones.shape[-1]
    aliased = result is not None

    def rows(lanes):
        return pl.BlockSpec((SPAN, lanes), lambda s, *_: (s, 0))

    def lanes():
        return pl.BlockSpec((LANES, SPAN), lambda s, *_: (0, s))

    operands = [pick, values, cum, bias, entry, end, keys, query, scores, ones, skip]
    in_specs = [
        ANY, rows(LANES), lanes(), rows(2 * LANES), rows(2 * LANES), lanes(), rows(LANES),
        pl.BlockSpec((1, SPAN, SPAN), lambda s, *_: (s, 0, 0)),
        whole((2 * LANES, width)), whole((1, width)),
    ]
    if aliased:
        operands.append(result)
        in_specs.append(ANY)
    return pl.pallas_call(
        functools.partial(
            layer_kernel, spans, first_head, heads, width // heads, lead, aliased
        ),
        grid_spec=pltpu.PrefetchScalarGridSpec(
            num_scalar_prefetch=1,
            grid=(spans,),
            in_specs=in_specs,
            out_specs=[
                pl.BlockSpec((SPAN, width), lambda s, *_: (s, column // width)),
                whole((LANES, width)),
            ],
            scratch_shapes=[
                pltpu.VMEM((tokens // SEG, SEG, width), bf16),
                pltpu.SemaphoreType.DMA((spans,)),
                pltpu.VMEM((SPAN, width), f32),
            ],
        ),
        out_shape=[
            jax.ShapeDtypeStruct((tokens, full), bf16),
            jax.ShapeDtypeStruct((LANES, width), f32),
        ],
        input_output_aliases={len(operands) - 1: 0} if aliased else {},
        compiler_params=params(),
        cost_estimate=pl.CostEstimate(
            flops=8 * tokens * SPAN * width, transcendentals=tokens * SPAN * heads,
            bytes_accessed=4 * tokens * width,
        ),
        name="layer",
    )(*operands)


def chunk_plan(heads):
    unit = heads // 10
    return ((4 * unit, 4 * unit), (0, 3 * unit), (8 * unit, 2 * unit), (3 * unit, unit))


def shifted(block, axis, distance):
    devices = range(lax.axis_size(axis))
    route = [(i - distance, i) for i in devices if i - distance in devices]
    return lax.ppermute(block, axis, route)


def on_device(
    token_rows, key_rows, query_rows, step_rows, decay_log, skip_gain, source_rows, document_starts
):
    tokens, full = token_rows.shape
    groups = lax.axis_size("dp")
    shards = lax.axis_size("seq")
    heads = decay_log.shape[0]
    head_width = full // heads
    runs = tokens // SEG
    capacity = runs // groups + 1
    pad = LANES - heads

    own = source_rows[0].reshape(runs, SEG)[:, 0][None, :] // SEG
    wanted = lax.all_to_all(
        jnp.broadcast_to(own, (groups, runs)), "dp", split_axis=0, concat_axis=0, tiled=True
    )
    me = lax.axis_index("dp").astype(jnp.int32)[None]
    send, pick = make_plan(groups, shards, runs, capacity, me, wanted, own)

    small = jnp.concatenate([key_rows, query_rows, jnp.pad(step_rows, ((0, 0), (0, pad)))], axis=1)
    small = small.reshape(runs, SEG, 3 * LANES)
    values = token_rows.reshape(runs, SEG, full)

    def exchange(block):
        got = lax.all_to_all(block, "dp", split_axis=0, concat_axis=0, tiled=True)
        return got.reshape(groups * capacity, SEG, block.shape[-1])

    blocks = [
        (first, count, first * head_width, count * head_width) for first, count in chunk_plan(heads)
    ]
    lead = 3 * LANES

    def gathered(number, token):
        _, _, column, width = blocks[number]
        if number == 0:
            parts = ((0, lead), (column, width))
            return collect(send, token, (small, values), parts, groups, capacity)
        return collect(send, token, (values,), ((column, width),), groups, capacity)

    lane_head = jnp.arange(full) // head_width
    ones = (jnp.arange(2 * LANES)[:, None] % LANES == lane_head[None, :]).astype(bf16)
    skip = jnp.repeat(skip_gain, head_width)[None, :]
    starts = document_starts[0] - lax.axis_index("seq").astype(jnp.int32) * tokens
    decay = jnp.pad(decay_log, (0, pad))[None, :]

    def entering_state(number, final):
        _, _, column, width = blocks[number]
        part = slice(column, column + width)
        entering = shifted(final.astype(bf16), "seq", 1)
        for hop in range(shards - 2):
            outgoing = through[:, part] * entering.astype(f32) + final
            entering = shifted(outgoing.astype(bf16), "seq", 1)
        return entering

    def corrected(result, number):
        _, _, column, width = blocks[number]
        return correct(
            result, entry, query, ones[:, column : column + width], incoming[number], column
        )

    sent = [gathered(0, send)]
    sent.append(gathered(1, sent[0]))
    result = None
    incoming = []
    waiting = []
    for number in range(len(blocks)):
        first_head, count, column, width = blocks[number]
        got = exchange(sent[number])
        if number == 0:
            prepared = prepare(pick, starts, got, decay, tokens)
            cum, bias, entry, end, through, keys, query, scores = prepared
            through = jnp.repeat(through[0, :heads], head_width)[None, :]
        part = slice(column, column + width)
        result, final = layer(
            result, pick, got, lead if number == 0 else 0,
            (cum, bias, entry, end, keys, query, scores),
            ones[:, part], skip[:, part], tokens, full, column, first_head, count,
        )
        incoming.append(entering_state(number, final))
        if number + 2 < len(blocks):
            sent.append(gathered(number + 2, final))
        if number == 1:
            result = corrected(result, 0)
    for number in range(1, len(blocks)):
        result = corrected(result, number)
    return result[None]


def solution(mesh):
    in_specs = (
        P(("dp", "seq"), None),
        P(("dp", "seq"), None),
        P(("dp", "seq"), None),
        P(("dp", "seq"), None),
        P(),
        P(),
        P("dp", "seq"),
        P("dp", None),
    )
    out_specs = P("dp", "seq", None)
    return jax.shard_map(
        on_device, mesh=mesh, in_specs=in_specs, out_specs=out_specs, check_vma=False
    )
```

```python
import functools

import jax
import jax.numpy as jnp
from jax import lax
from jax.experimental import pallas as pl
from jax.experimental.pallas import tpu as pltpu
from jax.sharding import PartitionSpec as P

SPAN = 256
SEG = 8
RUNS = SPAN // SEG
HALF = SPAN // 2
LANES = 128

f32, bf16 = jnp.float32, jnp.bfloat16
ANY = pl.BlockSpec(memory_space=pl.ANY)
VMEM_LIMIT = 60 * 1024 * 1024


def params(**more):
    return pltpu.CompilerParams(vmem_limit_bytes=VMEM_LIMIT, **more)


def whole(shape):
    return pl.BlockSpec(shape, lambda *_: (0,) * len(shape))


def spread(hilo, ones):
    return jnp.dot(hilo, ones, preferred_element_type=f32)


def split_float(value):
    high = value.astype(bf16)
    low = (value - high.astype(f32)).astype(bf16)
    return jnp.concatenate([high, low], axis=1)


def plan_kernel(groups, shards, runs, capacity, me_ref, wanted_ref, own_ref, send_ref, pick_ref):
    me = me_ref[0]
    earlier = lax.broadcasted_iota(jnp.int32, (runs, runs), 0) < lax.broadcasted_iota(
        jnp.int32, (runs, runs), 1
    )
    earlier = jnp.where(earlier, 1.0, 0.0).astype(bf16)

    def ranks(hit):
        ones = jnp.where(hit, 1.0, 0.0).astype(bf16)
        return jnp.dot(ones, earlier, preferred_element_type=f32).astype(jnp.int32)

    wanted = wanted_ref[...]
    mine = (wanted // runs) // shards == me
    local = wanted % runs
    rank = ranks(mine)
    lane = lax.broadcasted_iota(jnp.int32, (groups, LANES), 1)
    send = jnp.zeros((groups, LANES), jnp.int32)
    for slot in range(capacity):
        chosen = jnp.sum(jnp.where(mine & (rank == slot), local, 0), axis=1, keepdims=True)
        send = jnp.where(lane == slot, chosen, send)
    send_ref[...] = send
    source = (own_ref[...] // runs) // shards
    group = lax.broadcasted_iota(jnp.int32, (groups, runs), 0)
    hit = jnp.broadcast_to(source, (groups, runs)) == group
    pick_ref[...] = jnp.sum(
        jnp.where(hit, group * capacity + ranks(hit), 0), axis=0, keepdims=True
    )


def make_plan(groups, shards, runs, capacity, me, wanted, own):
    send, pick = pl.pallas_call(
        functools.partial(plan_kernel, groups, shards, runs, capacity),
        grid_spec=pltpu.PrefetchScalarGridSpec(
            num_scalar_prefetch=1,
            grid=(1,),
            in_specs=[whole((groups, runs)), whole((1, runs))],
            out_specs=[whole((groups, LANES)), whole((1, runs))],
        ),
        out_shape=[
            jax.ShapeDtypeStruct((groups, LANES), jnp.int32),
            jax.ShapeDtypeStruct((1, runs), jnp.int32),
        ],
        compiler_params=params(),
        name="plan",
    )(me, wanted, own)
    return send, pick[0]


def collect_kernel(groups, capacity, parts, send_ref, token_ref, *rest):
    sources = rest[: len(parts)]
    out_ref, held, gets, puts = rest[len(parts) :]

    def put(group):
        return pltpu.make_async_copy(held.at[group], out_ref.at[group], puts.at[group])

    for group in range(groups):

        @pl.loop(0, capacity)
        def _(slot):
            place = 0
            for source, (column, width) in zip(sources, parts):
                pltpu.make_async_copy(
                    source.at[send_ref[group, slot], :, pl.ds(column, width)],
                    held.at[group, slot, :, pl.ds(place, width)],
                    gets.at[group],
                ).start()
                place += width

    for group in range(groups):
        pltpu.make_async_copy(held.at[group], held.at[group], gets.at[group]).wait()
        put(group).start()
    for group in range(groups):
        put(group).wait()


def collect(send, token, sources, parts, groups, capacity):
    width = sum(part[1] for part in parts)
    return pl.pallas_call(
        functools.partial(collect_kernel, groups, capacity, parts),
        grid_spec=pltpu.PrefetchScalarGridSpec(
            num_scalar_prefetch=1,
            grid=(1,),
            in_specs=[ANY] * (1 + len(sources)),
            out_specs=ANY,
            scratch_shapes=[
                pltpu.VMEM((groups, capacity, SEG, width), bf16),
                pltpu.SemaphoreType.DMA((groups,)),
                pltpu.SemaphoreType.DMA((groups,)),
            ],
        ),
        out_shape=jax.ShapeDtypeStruct((groups, capacity, SEG, width), bf16),
        compiler_params=params(),
        cost_estimate=pl.CostEstimate(
            flops=0, transcendentals=0, bytes_accessed=4 * groups * capacity * SEG * width
        ),
        name="collect",
    )(send, token, *sources)


def fetch_spans(spans, column, width, pick_ref, source_ref, held, sems):
    @pl.when(pl.program_id(0) == 0)
    def _():
        @pl.loop(0, spans * RUNS)
        def _(run):
            pltpu.make_async_copy(
                source_ref.at[pick_ref[run], :, pl.ds(column, width)],
                held.at[run],
                sems.at[run // RUNS],
            ).start()


def fetched(held, sems, span):
    part = held.at[pl.ds(span * RUNS, RUNS)]
    pltpu.make_async_copy(part, part, sems.at[span]).wait()
    value = held[pl.ds(span * RUNS, RUNS)].astype(f32)
    return value.reshape(SPAN, value.shape[-1])


def prepare_kernel(
    spans, starts_count, pick_ref, starts_ref, small_ref, decay_ref,
    cum_ref, bias_ref, entry_ref, end_ref, through_ref, keys_ref, query_ref, score_ref,
    held, sems, later,
):
    step = pl.program_id(0)
    span = spans - 1 - step

    fetch_spans(spans, 0, 3 * LANES, pick_ref, small_ref, held, sems)

    @pl.when(step == 0)
    def _():
        later[...] = jnp.zeros_like(later)

    small = fetched(held, sems, span)
    keys = small[:, :LANES]
    query = small[:, LANES : 2 * LANES]
    raw = small[:, 2 * LANES :]
    steps = jnp.maximum(raw, 0.0) + jnp.log1p(jnp.exp(-jnp.abs(raw)))
    rate = jnp.exp(decay_ref[...])
    log_decay = -steps * rate
    row = lax.broadcasted_iota(jnp.int32, (SPAN, SPAN), 0)
    col = lax.broadcasted_iota(jnp.int32, (SPAN, SPAN), 1)
    lower = jnp.where(col <= row, 1.0, 0.0)
    cum = jnp.dot(lower, log_decay, precision=lax.Precision.HIGHEST, preferred_element_type=f32)
    low = span * SPAN
    doc_row = jnp.zeros((SPAN, SPAN), jnp.int32)
    doc_col = jnp.zeros((SPAN, SPAN), jnp.int32)
    doc = jnp.zeros((SPAN, LANES), jnp.int32)
    last = jnp.int32(0)
    after = jnp.int32(0)
    row_lanes = row[:, :LANES]
    for number in range(starts_count):
        start = starts_ref[number] - low
        inside = (start >= 0) & (start < SPAN)
        at = jnp.where(inside, start, jnp.int32(1 << 20))
        doc_row += (row >= at).astype(jnp.int32)
        doc_col += (col >= at).astype(jnp.int32)
        doc += (row_lanes >= at).astype(jnp.int32)
        last += inside.astype(jnp.int32)
        after += ((start >= SPAN) & (start < (spans - span) * SPAN)).astype(jnp.int32)
    linked = (doc_row == doc_col) & (col <= row)
    scores = lax.dot_general(
        query.astype(bf16), keys.astype(bf16), (((1,), (1,)), ((), ())), preferred_element_type=f32
    )
    score_ref[0] = jnp.where(linked, scores, 0.0)
    total = cum[SPAN - 1 :, :]
    to_end = total - cum
    entry_ref[...] = split_float(jnp.where(doc == 0, jnp.exp(cum), 0.0))
    at_end = doc == last
    end_ref[...] = split_float(jnp.where(at_end, jnp.exp(to_end), 0.0) * steps)
    cum_ref[...] = cum
    bias_ref[...] = (jnp.log(steps) - cum).T
    keys_ref[...] = keys.T.astype(bf16)
    query_ref[...] = query.astype(bf16)
    later[...] = later[...] + total
    through_ref[...] = jnp.where(last + after == 0, jnp.exp(later[...]), 0.0)


def prepare(pick, starts, small, decay, tokens):
    spans = tokens // SPAN
    starts_count = starts.shape[0]

    def back(step, *_):
        return (spans - 1 - step, 0)

    def back_lanes(step, *_):
        return (0, spans - 1 - step)

    def rows(width):
        return pl.BlockSpec((SPAN, width), back)

    return pl.pallas_call(
        functools.partial(prepare_kernel, spans, starts_count),
        grid_spec=pltpu.PrefetchScalarGridSpec(
            num_scalar_prefetch=2,
            grid=(spans,),
            in_specs=[ANY, whole((1, LANES))],
            out_specs=[
                rows(LANES),
                pl.BlockSpec((LANES, SPAN), back_lanes),
                rows(2 * LANES),
                rows(2 * LANES),
                whole((1, LANES)),
                pl.BlockSpec((LANES, SPAN), back_lanes),
                rows(LANES),
                pl.BlockSpec((1, SPAN, SPAN), lambda step, *_: (spans - 1 - step, 0, 0)),
            ],
            scratch_shapes=[
                pltpu.VMEM((tokens // SEG, SEG, 3 * LANES), bf16),
                pltpu.SemaphoreType.DMA((spans,)),
                pltpu.VMEM((1, LANES), f32),
            ],
        ),
        out_shape=[
            jax.ShapeDtypeStruct((tokens, LANES), f32),
            jax.ShapeDtypeStruct((LANES, tokens), f32),
            jax.ShapeDtypeStruct((tokens, 2 * LANES), bf16),
            jax.ShapeDtypeStruct((tokens, 2 * LANES), bf16),
            jax.ShapeDtypeStruct((1, LANES), f32),
            jax.ShapeDtypeStruct((LANES, tokens), bf16),
            jax.ShapeDtypeStruct((tokens, LANES), bf16),
            jax.ShapeDtypeStruct((spans, SPAN, SPAN), f32),
        ],
        compiler_params=params(),
        name="prepare",
    )(pick, starts, small, decay)


def correct_kernel(
    result_ref, entry_ref, query_ref, ones_ref, incoming_ref, out_ref, reach
):
    @pl.when(pl.program_id(0) == 0)
    def _():
        reach[...] = jnp.ones_like(reach)

    entry = spread(entry_ref[...], ones_ref[...]) * reach[...]
    from_state = jnp.dot(query_ref[...], incoming_ref[...], preferred_element_type=f32)
    out_ref[...] = (result_ref[...].astype(f32) + from_state * entry).astype(bf16)
    reach[...] = entry[SPAN - 1 :, :]


def correct(result, entry, query, ones, incoming, column):
    tokens, full = result.shape
    width = incoming.shape[-1]

    def rows(lanes, block=0):
        return pl.BlockSpec((SPAN, lanes), lambda s: (s, block))

    return pl.pallas_call(
        correct_kernel,
        grid=(tokens // SPAN,),
        in_specs=[
            rows(width, column // width), rows(2 * LANES), rows(LANES),
            whole((2 * LANES, width)), whole((LANES, width)),
        ],
        out_specs=rows(width, column // width),
        scratch_shapes=[pltpu.VMEM((1, width), f32)],
        out_shape=jax.ShapeDtypeStruct((tokens, full), bf16),
        input_output_aliases={0: 0},
        compiler_params=params(),
        cost_estimate=pl.CostEstimate(
            flops=6 * tokens * LANES * width, transcendentals=0, bytes_accessed=4 * tokens * width
        ),
        name="correct",
    )(result, entry, query, ones, incoming)


def layer_kernel(
    spans, first_head, heads, head_width, lead, aliased, pick_ref, values_ref, cum_ref, bias_ref, entry_ref,
    end_ref, keys_ref, query_ref, score_ref, ones_ref, skip_ref, *rest
):
    out_ref, state, held, sems, base = rest[1:] if aliased else rest
    span = pl.program_id(0)
    fetch_spans(spans, lead, heads * head_width, pick_ref, values_ref, held, sems)

    @pl.when(span == 0)
    def _():
        state[...] = jnp.zeros_like(state)

    values = fetched(held, sems, span)
    ones = ones_ref[...]
    entry = spread(entry_ref[...], ones)
    from_state = jnp.dot(query_ref[...], state[...].astype(bf16), preferred_element_type=f32)
    base[...] = from_state * entry + skip_ref[...] * values
    scaled = (values * spread(end_ref[...], ones)).astype(bf16)
    added = jnp.dot(keys_ref[...], scaled, preferred_element_type=f32)
    state[...] = entry[SPAN - 1 :, :] * state[...] + added
    packed = values.astype(bf16)
    per_tile = LANES // head_width
    lane = lax.broadcasted_iota(jnp.int32, (HALF, LANES), 1) // head_width
    for tile in range(heads // per_tile):
        columns = slice(tile * LANES, (tile + 1) * LANES)
        for half in range(2):
            rows = slice(half * HALF, (half + 1) * HALF)
            depth = (half + 1) * HALF
            scores = score_ref[0, rows, :depth]
            total = None
            for inner in range(per_tile):
                head = first_head + tile * per_tile + inner
                gap = cum_ref[rows, head : head + 1] + bias_ref[head : head + 1, :depth]
                weights = (scores * jnp.exp(jnp.minimum(gap, 60.0))).astype(bf16)
                part = jnp.dot(weights, packed[:depth, columns], preferred_element_type=f32)
                total = part if total is None else jnp.where(lane == inner, part, total)
            out_ref[rows, columns] = (base[rows, columns] + total).astype(bf16)


def layer(result, pick, values, lead, prepared, ones, skip, tokens, full, column, first_head, heads):
    cum, bias, entry, end, keys, query, scores = prepared
    spans = tokens // SPAN
    width = ones.shape[-1]
    aliased = result is not None

    def rows(lanes):
        return pl.BlockSpec((SPAN, lanes), lambda s, *_: (s, 0))

    def lanes():
        return pl.BlockSpec((LANES, SPAN), lambda s, *_: (0, s))

    operands = [pick, values, cum, bias, entry, end, keys, query, scores, ones, skip]
    in_specs = [
        ANY, rows(LANES), lanes(), rows(2 * LANES), rows(2 * LANES), lanes(), rows(LANES),
        pl.BlockSpec((1, SPAN, SPAN), lambda s, *_: (s, 0, 0)),
        whole((2 * LANES, width)), whole((1, width)),
    ]
    if aliased:
        operands.append(result)
        in_specs.append(ANY)
    return pl.pallas_call(
        functools.partial(
            layer_kernel, spans, first_head, heads, width // heads, lead, aliased
        ),
        grid_spec=pltpu.PrefetchScalarGridSpec(
            num_scalar_prefetch=1,
            grid=(spans,),
            in_specs=in_specs,
            out_specs=[
                pl.BlockSpec((SPAN, width), lambda s, *_: (s, column // width)),
                whole((LANES, width)),
            ],
            scratch_shapes=[
                pltpu.VMEM((tokens // SEG, SEG, width), bf16),
                pltpu.SemaphoreType.DMA((spans,)),
                pltpu.VMEM((SPAN, width), f32),
            ],
        ),
        out_shape=[
            jax.ShapeDtypeStruct((tokens, full), bf16),
            jax.ShapeDtypeStruct((LANES, width), f32),
        ],
        input_output_aliases={len(operands) - 1: 0} if aliased else {},
        compiler_params=params(),
        cost_estimate=pl.CostEstimate(
            flops=8 * tokens * SPAN * width, transcendentals=tokens * SPAN * heads,
            bytes_accessed=4 * tokens * width,
        ),
        name="layer",
    )(*operands)


def chunk_plan(heads):
    unit = heads // 4
    return ((0, unit), (2 * unit, 2 * unit), (unit, unit))


def shifted(block, axis, distance):
    devices = range(lax.axis_size(axis))
    route = [(i - distance, i) for i in devices if i - distance in devices]
    return lax.ppermute(block, axis, route)


def on_device(
    token_rows, key_rows, query_rows, step_rows, decay_log, skip_gain, source_rows, document_starts
):
    tokens, full = token_rows.shape
    groups = lax.axis_size("dp")
    shards = lax.axis_size("seq")
    heads = decay_log.shape[0]
    head_width = full // heads
    runs = tokens // SEG
    capacity = runs // groups + 1
    pad = LANES - heads

    own = source_rows[0].reshape(runs, SEG)[:, 0][None, :] // SEG
    wanted = lax.all_to_all(
        jnp.broadcast_to(own, (groups, runs)), "dp", split_axis=0, concat_axis=0, tiled=True
    )
    me = lax.axis_index("dp").astype(jnp.int32)[None]
    send, pick = make_plan(groups, shards, runs, capacity, me, wanted, own)

    small = jnp.concatenate([key_rows, query_rows, jnp.pad(step_rows, ((0, 0), (0, pad)))], axis=1)
    small = small.reshape(runs, SEG, 3 * LANES)
    values = token_rows.reshape(runs, SEG, full)

    def exchange(block):
        got = lax.all_to_all(block, "dp", split_axis=0, concat_axis=0, tiled=True)
        return got.reshape(groups * capacity, SEG, block.shape[-1])

    blocks = [
        (first, count, first * head_width, count * head_width) for first, count in chunk_plan(heads)
    ]
    lead = 3 * LANES

    def gathered(number, token):
        _, _, column, width = blocks[number]
        if number == 0:
            parts = ((0, lead), (column, width))
            return collect(send, token, (small, values), parts, groups, capacity)
        return collect(send, token, (values,), ((column, width),), groups, capacity)

    lane_head = jnp.arange(full) // head_width
    ones = (jnp.arange(2 * LANES)[:, None] % LANES == lane_head[None, :]).astype(bf16)
    skip = jnp.repeat(skip_gain, head_width)[None, :]
    starts = document_starts[0] - lax.axis_index("seq").astype(jnp.int32) * tokens
    decay = jnp.pad(decay_log, (0, pad))[None, :]

    def entering_state(number, final):
        _, _, column, width = blocks[number]
        part = slice(column, column + width)
        entering = shifted(final.astype(bf16), "seq", 1)
        for hop in range(shards - 2):
            outgoing = through[:, part] * entering.astype(f32) + final
            entering = shifted(outgoing.astype(bf16), "seq", 1)
        return entering

    def corrected(result, number):
        _, _, column, width = blocks[number]
        return correct(
            result, entry, query, ones[:, column : column + width], incoming[number], column
        )

    sent = [gathered(0, send)]
    sent.append(gathered(1, sent[0]))
    result = None
    incoming = []
    waiting = []
    for number in range(len(blocks)):
        first_head, count, column, width = blocks[number]
        got = exchange(sent[number])
        if number == 0:
            prepared = prepare(pick, starts, got, decay, tokens)
            cum, bias, entry, end, through, keys, query, scores = prepared
            through = jnp.repeat(through[0, :heads], head_width)[None, :]
        part = slice(column, column + width)
        result, final = layer(
            result, pick, got, lead if number == 0 else 0,
            (cum, bias, entry, end, keys, query, scores),
            ones[:, part], skip[:, part], tokens, full, column, first_head, count,
        )
        incoming.append(entering_state(number, final))
        if number + 2 < len(blocks):
            sent.append(gathered(number + 2, final))
        if number == 0:
            result = corrected(result, 0)
    for number in range(1, len(blocks)):
        result = corrected(result, number)
    return result[None]


def solution(mesh):
    in_specs = (
        P(("dp", "seq"), None),
        P(("dp", "seq"), None),
        P(("dp", "seq"), None),
        P(("dp", "seq"), None),
        P(),
        P(),
        P("dp", "seq"),
        P("dp", None),
    )
    out_specs = P("dp", "seq", None)
    return jax.shard_map(
        on_device, mesh=mesh, in_specs=in_specs, out_specs=out_specs, check_vma=False
    )
```
